32 devices in a mesh: pipe: 4 (over z), seq: 2 (over core), tp: 4 (over y, x).
Axes of the slice: x: 2, y: 2, z: 4, core: 2. Of those that a mesh axis runs over, the one named last changes fastest.
Arguments:
- in_flight: bfloat16 [4, 128, 4096], P('pipe', 'tp', 'seq'), may hold values from -15 to 15
- arriving: bfloat16 [1, 128, 4096], P(None, 'tp', 'seq'), may hold values from -15 to 15
- norm_gain: bfloat16 [4, 4096], P('pipe', 'seq'), may hold values from 0.099609375 to 1.8984375
- gate_weight: bfloat16 [4, 4096, 5504], P('pipe', 'seq', 'tp'), may hold values from -0.09375 to 0.09375
- up_weight: bfloat16 [4, 4096, 5504], P('pipe', 'seq', 'tp'), may hold values from -0.09375 to 0.09375
- down_weight: bfloat16 [4, 5504, 4096], P('pipe', 'tp', 'seq'), may hold values from -0.078125 to 0.078125
Outputs:
- produced: bfloat16 [2, 4, 128, 4096], P(None, 'pipe', 'tp', 'seq')
The draws below stay inside these ranges and needn't reach their ends.
All inputs are finite; a program needn't handle non-finite values.
Results may differ from the reference program's by a relative error of at most 0.015.
Values may be sent and summed in bfloat16 or wider, within the bound.
A program may use at most 64 MiB of HBM per device.

```python
import jax
import jax.numpy as jnp
from jax import lax

D = 4096
FFW = 5504
TICKS = 2
SECTIONS = 4
MB_TOK = 128
N_TP = 4


def activations(key, shape, salt):
    first, second = jax.random.split(jax.random.fold_in(key, salt), 2)
    ramp = jnp.exp(jnp.linspace(jnp.log(0.6), jnp.log(1.8), D)).astype(jnp.float32)
    columns = ramp * jax.random.uniform(second, (D,), jnp.float32, 0.7, 1.3)
    base = jnp.clip(jax.random.normal(first, shape, jnp.float32), -6.0, 6.0)
    values = base * columns
    return jnp.clip(values, -15.0, 15.0)


def draw_in_flight(key, part):
    return activations(key, (SECTIONS, MB_TOK, D), 101).astype(jnp.bfloat16)


def draw_arriving(key, part):
    return activations(key, (TICKS - 1, MB_TOK, D), 202).astype(jnp.bfloat16)


def block_levels(rng, extent, cuts, smallest, largest):
    def one(position, blocks):
        draws = jax.random.uniform(jax.random.fold_in(jax.random.fold_in(rng, 6), position), (blocks,), jnp.float32, smallest / len(cuts), largest / len(cuts))
        return jnp.repeat(jnp.exp(draws), extent[position] // blocks).reshape((-1,) + (1,) * (len(extent) - position - 1))

    level = one(*cuts[0])
    for cut in cuts[1:]:
        level = level * one(*cut)
    return level


def normal_values(key, extent, spread, most, cuts=(), kind=jnp.bfloat16):
    result = jax.random.normal(key, extent, jnp.float32) * spread
    if len(cuts) > 0:
        result = block_levels(key, extent, cuts, -0.22, 0.18) * result
    return jnp.clip(result, min=-most, max=most).astype(kind)


def setup_inputs(seed: int = 0) -> dict:
    streams_of = jax.random.split(jax.random.key(seed), 7)
    return {
        "in_flight": draw_in_flight(jax.random.fold_in(streams_of[6], 71), 0),
        "arriving": draw_arriving(jax.random.fold_in(streams_of[6], 71), 0),
        "norm_gain": jnp.clip(1.0 + 0.18 * jax.random.normal(streams_of[2], (SECTIONS, D), jnp.float32), 0.099609375, 1.8984375).astype(jnp.bfloat16),
        "gate_weight": normal_values(streams_of[3], (SECTIONS, D, FFW), D ** -0.5, 0.09375, ((0, 4), (1, 2), (2, 4))),
        "up_weight": normal_values(streams_of[4], (SECTIONS, D, FFW), D ** -0.5, 0.09375, ((0, 4), (1, 2), (2, 4))),
        "down_weight": normal_values(streams_of[5], (SECTIONS, FFW, D), FFW ** -0.5, 0.078125, ((0, 4), (1, 4), (2, 2))),
    }


epsilon = 1e-05

def section_layer(x, gain, gate_w, up_w, down_w):
    wide = x.astype(jnp.float32)
    squares = lax.optimization_barrier(jnp.sum(wide * wide, axis=1))
    inverse = lax.rsqrt(squares / D + epsilon)[:, None]
    scaled = (wide * gain.astype(jnp.float32)[None, :]).astype(jnp.bfloat16)
    gate = jnp.dot(scaled, gate_w, preferred_element_type=jnp.float32) * inverse
    up_val = jnp.dot(scaled, up_w, preferred_element_type=jnp.float32) * inverse
    hidden = (jax.nn.silu(gate) * up_val).astype(jnp.bfloat16)
    block_width = FFW // N_TP

    def add_block(total, block_index):
        start = (block_index * block_width).astype(jnp.int32)
        hidden_block = lax.dynamic_slice_in_dim(hidden, start, block_width, 1)
        weight_block = lax.dynamic_slice_in_dim(down_w, start, block_width, 0)
        partial_sum = jnp.dot(hidden_block, weight_block, preferred_element_type=jnp.float32)
        rounded = lax.optimization_barrier(partial_sum.astype(jnp.bfloat16))
        return (total + rounded.astype(jnp.float32), None)
    initial = jnp.zeros((x.shape[0], D), jnp.float32)
    branch, _ = lax.scan(add_block, initial, jnp.arange(N_TP, dtype=jnp.int32))
    return (wide + branch).astype(jnp.bfloat16)

def reference(in_flight, arriving, norm_gain, gate_weight, up_weight, down_weight):
    current = in_flight
    results = []
    for tick in range(TICKS):
        produced_now = lax.map(lambda items: section_layer(*items), (current, norm_gain, gate_weight, up_weight, down_weight))
        results.append(produced_now)
        if tick + 1 < TICKS:
            current = jnp.concatenate([arriving[tick][None], produced_now[:-1]], axis=0)
    return jnp.stack(results)
```

```python
import functools

import jax
import jax.numpy as jnp
from jax import lax
from jax.experimental import pallas as pl
from jax.experimental.pallas import tpu as pltpu
from jax.sharding import PartitionSpec as P

epsilon = 1e-05
MESH = pl.DeviceIdType.MESH
F32, BF16 = jnp.float32, jnp.bfloat16


def pieces(total, step):
    return [(at, min(step, total - at)) for at in range(0, total, step)]


def times(a, b):
    return lax.dot_general(a, b, (((1,), (1,)), ((), ())), preferred_element_type=F32)


def partner(me, k, n):
    if n & (n - 1):
        raise ValueError("axis size")
    result, bit = 0, 1
    while bit < n:
        digit = (me // bit) % 2
        if k & bit:
            digit = 1 - digit
        result = result + digit * bit
        bit *= 2
    return result


def body(cfg, *refs):
    T, R, DL, F, J, CW, NP, NS, NT, hidden_parts = cfg
    NF = len(hidden_parts)
    M = R * NT
    refs = list(refs)
    in_flight, arriving, gain, gate_w, up_w, down_w, out = refs[:7]
    (xin, xg, gate_v, up_v, down_v, acc_g, acc_u, acc_y, sq, sq_recv, rs_send, rs_recv, made) = refs[7:20]
    ex_send = refs[20:20 + NF]
    ex_recv = refs[20 + NF:20 + 2 * NF]
    (w_sem, d_sem, x_sem, z_sem, ag_s, ag_r, rs_s, rs_r, sq_s, sq_r, ex_s, ex_r) = refs[20 + 2 * NF:]

    pipe, seq, tp = lax.axis_index("pipe"), lax.axis_index("seq"), lax.axis_index("tp")
    width = DL * NS

    def remote(src, dst, send, recv, where):
        return pltpu.make_async_remote_copy(
            src_ref=src, dst_ref=dst, send_sem=send, recv_sem=recv, device_id=where, device_id_type=MESH
        )

    def await_local(ref, sem):
        pltpu.make_async_copy(ref, ref, sem).wait()

    for j in range(J):
        pltpu.make_async_copy(in_flight.at[0, :, pl.ds(j * CW, CW)], xin.at[0, j], x_sem.at[0, j]).start()

    @pl.when(pipe == 0)
    def _():
        for t in range(1, T):
            for j in range(J):
                pltpu.make_async_copy(
                    arriving.at[t - 1, :, pl.ds(j * CW, CW)], xin.at[t, j], x_sem.at[t, j]
                ).start()

    for j in range(J):
        for which, (src, dst) in enumerate(((gate_w, gate_v), (up_w, up_v))):
            pltpu.make_async_copy(src.at[0, :, pl.ds(j * CW, CW)], dst.at[j], w_sem.at[which, j]).start()
    for n, (at, size) in enumerate(hidden_parts):
        pltpu.make_async_copy(down_w.at[0, pl.ds(at, size), :], down_v.at[pl.ds(at, size), :], d_sem.at[n]).start()

    barrier = pltpu.get_barrier_semaphore()
    for k in range(1, NT):
        pl.semaphore_signal(barrier, inc=1, device_id={"tp": partner(tp, k, NT)}, device_id_type=MESH)
    for k in range(1, NS):
        pl.semaphore_signal(barrier, inc=1, device_id={"seq": partner(seq, k, NS)}, device_id_type=MESH)

    @pl.when(pipe > 0)
    def _():
        pl.semaphore_signal(barrier, inc=1, device_id={"pipe": pipe - 1}, device_id_type=MESH)

    peers = NT - 1 + NS - 1

    @pl.when(pipe < NP - 1)
    def _():
        pl.semaphore_wait(barrier, peers + 1)

    @pl.when(pipe == NP - 1)
    def _():
        pl.semaphore_wait(barrier, peers)

    def gather_copy(t, j, k):
        return remote(
            xin.at[t, j], xg.at[t, j, pl.ds(k * R, R), :], ag_s.at[t, j, k - 1], ag_r.at[t, j, k - 1],
            {"tp": partner(tp, k, NT)},
        )

    def spread(t, j):
        await_local(xin.at[t, j], x_sem.at[t, j])
        for k in reversed(range(1, NT)):
            gather_copy(t, j, k).start()
        xg[t, j, 0:R, :] = xin[t, j]

    def shift_copy(t, j):
        return remote(made.at[t, j], xin.at[t + 1, j], z_sem.at[t, j], x_sem.at[t + 1, j], {"pipe": pipe + 1})

    def scatter_copy(t, j, k):
        return remote(
            rs_send.at[t, j, pl.ds(k * R, R), :], rs_recv.at[t, j, k - 1], rs_s.at[t, j, k - 1],
            rs_r.at[t, j, k - 1], {"tp": partner(tp, k, NT)},
        )

    def squares_copy(t, k):
        return remote(sq.at[t], sq_recv.at[t, k - 1], sq_s.at[t, k - 1], sq_r.at[t, k - 1], {"seq": partner(seq, k, NS)})

    def exchange_copy(t, n, k):
        return remote(
            ex_send[n].at[t], ex_recv[n].at[t, k - 1], ex_s.at[t, n, k - 1], ex_r.at[t, n, k - 1],
            {"seq": partner(seq, k, NS)},
        )

    for j in range(J):
        spread(0, j)

    def tick(t, carry):
        acc_g[...] = jnp.zeros_like(acc_g)
        acc_u[...] = jnp.zeros_like(acc_u)
        sq[t] = jnp.zeros((M, 128), F32)

        def arrive(j):
            for k in range(1, NT):
                await_local(xg.at[t, j, pl.ds(k * R, R), :], ag_r.at[t, j, k - 1])

            @pl.when(t == 0)
            def _():
                await_local(gate_v.at[j], w_sem.at[0, j])
                await_local(up_v.at[j], w_sem.at[1, j])

            wide = xg[t, j].astype(F32)
            scaled = (wide * gain[:, pl.ds(pl.multiple_of(j * CW, CW), CW)].astype(F32)).astype(BF16)
            square = wide * wide
            total = sq[t]
            for at in range(0, CW, 128):
                total = total + square[:, at:at + 128]
            sq[t] = total
            return scaled

        def some(j, c):
            scaled = arrive(j)
            for at, size in pieces(F, 256):
                for weight, acc in ((gate_v, acc_g), (up_v, acc_u)):
                    acc[:, at:at + size] += times(scaled, weight[j, at:at + size, :])
            return c

        if J > 1:
            lax.fori_loop(0, J - 1, some, 0)
        scaled = arrive(J - 1)
        for k in range(1, NS):
            squares_copy(t, k).start()
        for n, (base, length) in enumerate(hidden_parts):
            for at, size in pieces(length, 256):
                for which, (weight, acc) in enumerate(((gate_v, acc_g), (up_v, acc_u))):
                    value = acc[:, base + at:base + at + size] + times(
                        scaled, weight[J - 1, base + at:base + at + size, :]
                    )
                    acc[:, base + at:base + at + size] = value
                    ex_send[n][t, which, :, at:at + size] = value.astype(BF16)
            for k in range(1, NS):
                exchange_copy(t, n, k).start()

        total = sq[t]
        for k in range(1, NS):
            await_local(sq_recv.at[t, k - 1], sq_r.at[t, k - 1])
            total = total + sq_recv[t, k - 1]
        inverse = lax.rsqrt(jnp.sum(total, axis=1, keepdims=True) / width + epsilon)

        for n, (base, length) in enumerate(hidden_parts):
            for k in range(1, NS):
                await_local(ex_recv[n].at[t, k - 1], ex_r.at[t, n, k - 1])

            @pl.when(t == 0)
            def _():
                await_local(down_v.at[pl.ds(base, length), :], d_sem.at[n])

            gate = acc_g[:, base:base + length]
            up = acc_u[:, base:base + length]
            for k in range(1, NS):
                gate = gate + ex_recv[n][t, k - 1, 0].astype(F32)
                up = up + ex_recv[n][t, k - 1, 1].astype(F32)
            hidden = (jax.nn.silu(gate * inverse) * (up * inverse)).astype(BF16)
            last = n == NF - 1
            for j in range(J):
                for at, size in pieces(CW, 256):
                    lo = j * CW + at
                    value = jnp.dot(hidden, down_v[base:base + length, lo:lo + size], preferred_element_type=F32)
                    if n > 0:
                        value = value + acc_y[:, lo:lo + size]
                    if last:
                        rs_send[t, j, :, at:at + size] = value.astype(BF16)
                    else:
                        acc_y[:, lo:lo + size] = value
                if last:
                    for k in reversed(range(1, NT)):
                        scatter_copy(t, j, k).start()

        def finish(j):
            branch = rs_send[t, j, 0:R, :].astype(F32)
            for k in range(1, NT):
                await_local(rs_recv.at[t, j, k - 1], rs_r.at[t, j, k - 1])
                branch = branch + rs_recv[t, j, k - 1].astype(F32)
            produced = (xin[t, j].astype(F32) + branch).astype(BF16)
            out[t, :, j * CW:(j + 1) * CW] = produced

            @pl.when((t < T - 1) & (pipe < NP - 1))
            def _():
                made[t, j] = produced
                shift_copy(t, j).start()

        for j in range(J):
            finish(j)
            if j > 0:
                @pl.when(t < T - 1)
                def _():
                    spread(t + 1, j - 1)

        @pl.when(t < T - 1)
        def _():
            spread(t + 1, J - 1)

        return carry

    lax.fori_loop(0, T, tick, 0)

    def sent(t, carry):
        for j in range(J):
            for k in range(1, NT):
                gather_copy(t, j, k).wait_send()
                scatter_copy(t, j, k).wait_send()

            @pl.when((t < T - 1) & (pipe < NP - 1))
            def _():
                shift_copy(t, j).wait_send()
        for k in range(1, NS):
            squares_copy(t, k).wait_send()
            for n in range(NF):
                exchange_copy(t, n, k).wait_send()
        return carry

    lax.fori_loop(0, T, sent, 0)


def solution(mesh):
    NP, NS, NT = mesh.shape["pipe"], mesh.shape["seq"], mesh.shape["tp"]

    def shards(in_flight, arriving, norm_gain, gate_weight, up_weight, down_weight):
        T = arriving.shape[0] + 1
        R, DL = in_flight.shape[1:]
        F = gate_weight.shape[2]
        CW = min(512, DL)
        J = DL // CW
        M = R * NT
        parts = pieces(F, 512)
        NF = len(parts)
        cfg = (T, R, DL, F, J, CW, NP, NS, NT, parts)
        hbm = pl.BlockSpec(memory_space=pltpu.HBM)
        vmem = pl.BlockSpec(memory_space=pltpu.VMEM)
        dma = pltpu.SemaphoreType.DMA
        ps = max(NS - 1, 1)
        scratch = [
            pltpu.VMEM((T, J, R, CW), BF16),
            pltpu.VMEM((T, J, M, CW), BF16),
            pltpu.VMEM((J, F, CW), BF16),
            pltpu.VMEM((J, F, CW), BF16),
            pltpu.VMEM((F, DL), BF16),
            pltpu.VMEM((M, F), F32),
            pltpu.VMEM((M, F), F32),
            pltpu.VMEM((M, DL), F32),
            pltpu.VMEM((T, M, 128), F32),
            pltpu.VMEM((T, ps, M, 128), F32),
            pltpu.VMEM((T, J, M, CW), BF16),
            pltpu.VMEM((T, J, NT - 1, R, CW), BF16),
            pltpu.VMEM((T, J, R, CW), BF16),
        ]
        scratch += [pltpu.VMEM((T, 2, M, size), BF16) for _, size in parts]
        scratch += [pltpu.VMEM((T, ps, 2, M, size), BF16) for _, size in parts]
        scratch += [
            dma((2, J)), dma((NF,)), dma((T, J)), dma((T, J)),
            dma((T, J, NT - 1)), dma((T, J, NT - 1)), dma((T, J, NT - 1)), dma((T, J, NT - 1)),
            dma((T, ps)), dma((T, ps)), dma((T, NF, ps)), dma((T, NF, ps)),
        ]
        flops = 2 * T * M * DL * F * 3
        made = pl.pallas_call(
            functools.partial(body, cfg),
            out_shape=pltpu.VMEM((T, R, DL), BF16),
            in_specs=[hbm, hbm, vmem, hbm, hbm, hbm],
            out_specs=vmem,
            scratch_shapes=scratch,
            compiler_params=pltpu.CompilerParams(
                collective_id=0, has_side_effects=True, vmem_limit_bytes=56 * 1024 * 1024
            ),
            cost_estimate=pl.CostEstimate(flops=flops, bytes_accessed=6 * DL * F, transcendentals=T * M * F),
            name="relay",
        )(in_flight, arriving, norm_gain, jnp.swapaxes(gate_weight, 1, 2), jnp.swapaxes(up_weight, 1, 2), down_weight)
        return made[:, None]

    placed = (
        P("pipe", "tp", "seq"),
        P(None, "tp", "seq"),
        P("pipe", "seq"),
        P("pipe", "seq", "tp"),
        P("pipe", "seq", "tp"),
        P("pipe", "tp", "seq"),
    )
    return jax.shard_map(
        shards, mesh=mesh, in_specs=placed, out_specs=P(None, "pipe", "tp", "seq"), check_vma=False
    )
```

```python
import functools

import jax
import jax.numpy as jnp
from jax import lax
from jax.experimental import pallas as pl
from jax.experimental.pallas import tpu as pltpu
from jax.sharding import PartitionSpec as P

epsilon = 1e-05
MESH = pl.DeviceIdType.MESH
F32, BF16 = jnp.float32, jnp.bfloat16
COLUMNS = 512
PART = 512
BEFORE = 1


def pieces(total, step):
    return [(at, min(step, total - at)) for at in range(0, total, step)]


def times(a, b):
    return lax.dot_general(a, b, (((1,), (1,)), ((), ())), preferred_element_type=F32)


def partner(me, k, n):
    if n & (n - 1):
        raise ValueError("axis size")
    result, bit = 0, 1
    while bit < n:
        digit = (me // bit) % 2
        if k & bit:
            digit = 1 - digit
        result = result + digit * bit
        bit *= 2
    return result


def body(cfg, *refs):
    T, R, DL, F, CW, H, NP, NS, NT, parts = cfg
    J, RH, NF = DL // CW, R // H, len(parts)
    M = RH * NT
    refs = list(refs)
    in_flight, arriving, gain_in, gate_w, up_w, down_w, out = refs[:7]
    (gain, xg, gate_v, up_v, gate_t, up_t, down_v, acc_g, acc_u, acc_y, sq, sq_recv, rs_send, rs_recv) = refs[7:21]
    ex_send = refs[21:21 + NF]
    ex_recv = refs[21 + NF:21 + 2 * NF]
    (g_sem, w_sem, d_sem, x_sem, z_sem, ag_s, ag_r, rs_s, rs_r, sq_s, sq_r, ex_s, ex_r) = refs[21 + 2 * NF:]

    pipe, seq, tp = lax.axis_index("pipe"), lax.axis_index("seq"), lax.axis_index("tp")
    width = DL * NS

    def remote(src, dst, send, recv, where):
        return pltpu.make_async_remote_copy(
            src_ref=src, dst_ref=dst, send_sem=send, recv_sem=recv, device_id=where, device_id_type=MESH
        )

    def await_bytes(ref, sem):
        pltpu.make_async_copy(ref, ref, sem).wait()

    def own(t, h, j):
        return xg.at[t, j, 0, h]

    def others(t, h, j):
        return xg.at[t, j, pl.ds(1, NT - 1), h]

    for j in range(J):
        for h in range(H):
            pltpu.make_async_copy(
                in_flight.at[0, pl.ds(h * RH, RH), pl.ds(j * CW, CW)], own(0, h, j), x_sem.at[0, h, j]
            ).start()
    pltpu.make_async_copy(gain_in, gain, g_sem).start()
    for j in range(J):
        for which, (src, dst) in enumerate(((gate_w, gate_v), (up_w, up_v))):
            pltpu.make_async_copy(src.at[0, :, pl.ds(j * CW, CW)], dst.at[j], w_sem.at[which, j]).start()
    for n, (at, size) in enumerate(parts):
        pltpu.make_async_copy(down_w.at[0, pl.ds(at, size), :], down_v.at[pl.ds(at, size), :], d_sem.at[n]).start()

    @pl.when(pipe == 0)
    def _():
        for t in range(1, T):
            for h in range(H):
                for j in range(J):
                    pltpu.make_async_copy(
                        arriving.at[t - 1, pl.ds(h * RH, RH), pl.ds(j * CW, CW)], own(t, h, j), x_sem.at[t, h, j]
                    ).start()

    barrier = pltpu.get_barrier_semaphore()
    for k in range(1, NT):
        pl.semaphore_signal(barrier, inc=1, device_id={"tp": partner(tp, k, NT)}, device_id_type=MESH)
    for k in range(1, NS):
        pl.semaphore_signal(barrier, inc=1, device_id={"seq": partner(seq, k, NS)}, device_id_type=MESH)

    @pl.when(pipe > 0)
    def _():
        pl.semaphore_signal(barrier, inc=1, device_id={"pipe": pipe - 1}, device_id_type=MESH)

    peers = NT - 1 + NS - 1

    @pl.when(pipe < NP - 1)
    def _():
        pl.semaphore_wait(barrier, peers + 1)

    @pl.when(pipe == NP - 1)
    def _():
        pl.semaphore_wait(barrier, peers)

    def spread(t, h, j):
        await_bytes(own(t, h, j), x_sem.at[t, h, j])
        for k in reversed(range(1, NT)):
            remote(
                own(t, h, j), xg.at[t, j, k, h], ag_s.at[t, h, j], ag_r.at[t, h, j], {"tp": partner(tp, k, NT)}
            ).start()

    def spread_all(t, j):
        for h in range(H):
            await_bytes(own(t, h, j), x_sem.at[t, h, j])
        for k in reversed(range(1, NT)):
            remote(
                xg.at[t, j, 0], xg.at[t, j, k], ag_s.at[t, 0, j], ag_r.at[t, 0, j], {"tp": partner(tp, k, NT)}
            ).start()

    def shift_copy(t, h, j):
        return remote(
            out.at[t, pl.ds(h * RH, RH), pl.ds(j * CW, CW)], own(t + 1, h, j), z_sem.at[t, h, j],
            x_sem.at[t + 1, h, j], {"pipe": pipe + 1},
        )

    def squares_copy(t, h, k):
        return remote(
            sq.at[t, h], sq_recv.at[t, h, k - 1], sq_s.at[t, h, k - 1], sq_r.at[t, h, k - 1],
            {"seq": partner(seq, k, NS)},
        )

    def exchange_copy(t, h, n, k):
        return remote(
            ex_send[n].at[t, h], ex_recv[n].at[t, h, k - 1], ex_s.at[t, h, n, k - 1], ex_r.at[t, h, n, k - 1],
            {"seq": partner(seq, k, NS)},
        )

    def scale(x, j):
        wide = x.astype(F32)
        scaled = (wide * gain[:, pl.ds(pl.multiple_of(j * CW, CW), CW)].astype(F32)).astype(BF16)
        square = wide * wide
        total = square[:, 0:128]
        for at in range(128, CW, 128):
            total = total + square[:, at:at + 128]
        return scaled, total

    def turn(j):
        for which, (raw, turned) in enumerate(((gate_v, gate_t), (up_v, up_t))):
            for at in range(0, CW, 256):
                turned[j, at:at + 256, :] = jnp.transpose(raw[j, :, at:at + 256])

    def arrive_all(t, j):
        await_bytes(xg.at[t, j, pl.ds(1, NT - 1)], ag_r.at[t, 0, j])
        scaled, total = scale(xg[t, j].reshape(H * M, CW), j)
        total = total.reshape(NT, H, RH, 128)
        for h in range(H):
            sq[t, h] += total[:, h].reshape(M, 128)
        return scaled

    def arrive(t, h, j):
        await_bytes(others(t, h, j), ag_r.at[t, h, j])
        scaled, total = scale(xg[t, j, :, h].reshape(M, CW), j)
        sq[t, h] += total
        return scaled

    kinds = ((gate_t, acc_g), (up_t, acc_u))
    raws = ((gate_v, acc_g), (up_v, acc_u))

    def loaded(j):
        await_bytes(gate_v.at[j], w_sem.at[0, j])
        await_bytes(up_v.at[j], w_sem.at[1, j])

    def clear(t):
        acc_g[...] = jnp.zeros_like(acc_g)
        acc_u[...] = jnp.zeros_like(acc_u)
        for h in range(H):
            sq[t, h] = jnp.zeros((M, 128), F32)

    def project_all(t, j):
        scaled = arrive_all(t, j)
        for at, size in pieces(F, 256):
            for weight, acc in raws:
                acc[:, :, :, at:at + size] += times(scaled, weight[j, at:at + size, :]).reshape(NT, H, RH, size)

    def project(t, h, j):
        scaled = arrive(t, h, j)
        for at, size in pieces(F, 256):
            for weight, acc in kinds:
                acc[:, h, :, at:at + size] += jnp.dot(
                    scaled, weight[j, :, at:at + size], preferred_element_type=F32
                ).reshape(NT, RH, size)

    def last_all(t):
        scaled = arrive_all(t, J - 1)
        for h in range(H):
            for k in range(1, NS):
                squares_copy(t, h, k).start()
        for n, (base, length) in enumerate(parts):
            for at, size in pieces(length, 256):
                lo, hi = base + at, base + at + size
                for which, (weight, acc) in enumerate(raws):
                    value = acc[:, :, :, lo:hi] + times(scaled, weight[J - 1, lo:hi, :]).reshape(NT, H, RH, size)
                    acc[:, :, :, lo:hi] = value
                    rounded = value.astype(BF16)
                    for h in range(H):
                        ex_send[n][t, h, which, :, at:at + size] = rounded[:, h].reshape(M, size)
            for h in range(H):
                for k in range(1, NS):
                    exchange_copy(t, h, n, k).start()

    def project_last(t, h):
        scaled = arrive(t, h, J - 1)
        for k in range(1, NS):
            squares_copy(t, h, k).start()
        for n, (base, length) in enumerate(parts):
            for at, size in pieces(length, 256):
                lo, hi = base + at, base + at + size
                for which, (weight, acc) in enumerate(kinds):
                    value = acc[:, h, :, lo:hi].reshape(M, size) + jnp.dot(
                        scaled, weight[J - 1, :, lo:hi], preferred_element_type=F32
                    )
                    acc[:, h, :, lo:hi] = value.reshape(NT, RH, size)
                    ex_send[n][t, h, which, :, at:at + size] = value.astype(BF16)
            for k in range(1, NS):
                exchange_copy(t, h, n, k).start()

    def contract(t, h):
        total = sq[t, h]
        for k in range(1, NS):
            await_bytes(sq_recv.at[t, h, k - 1], sq_r.at[t, h, k - 1])
            total = total + sq_recv[t, h, k - 1]
        inverse = lax.rsqrt(jnp.sum(total, axis=1, keepdims=True) / width + epsilon)
        for n, (base, length) in enumerate(parts):
            for k in range(1, NS):
                await_bytes(ex_recv[n].at[t, h, k - 1], ex_r.at[t, h, n, k - 1])
            if h == 0 and isinstance(t, int):
                await_bytes(down_v.at[pl.ds(base, length), :], d_sem.at[n])
            gate = acc_g[:, h, :, base:base + length].reshape(M, length)
            up = acc_u[:, h, :, base:base + length].reshape(M, length)
            for k in range(1, NS):
                gate = gate + ex_recv[n][t, h, k - 1, 0].astype(F32)
                up = up + ex_recv[n][t, h, k - 1, 1].astype(F32)
            hidden = (jax.nn.silu(gate * inverse) * (up * inverse)).astype(BF16)
            last = n == NF - 1
            for j in range(J):
                for at, size in pieces(CW, 256):
                    lo = j * CW + at
                    value = jnp.dot(hidden, down_v[base:base + length, lo:lo + size], preferred_element_type=F32)
                    if n > 0:
                        value = value + acc_y[:, lo:lo + size]
                    if last:
                        rs_send[t, h, j, :, at:at + size] = value.astype(BF16)
                    else:
                        acc_y[:, lo:lo + size] = value
                if last:
                    for k in reversed(range(1, NT)):
                        remote(
                            rs_send.at[t, h, j, pl.ds(k * RH, RH), :], rs_recv.at[t, h, j, pl.ds((k - 1) * RH, RH), :],
                            rs_s.at[t, h, j], rs_r.at[t, h, j], {"tp": partner(tp, k, NT)},
                        ).start()

    def finish(t, h, j):
        await_bytes(rs_recv.at[t, h, j], rs_r.at[t, h, j])
        branch = rs_send[t, h, j, 0:RH, :].astype(F32)
        for k in range(1, NT):
            branch = branch + rs_recv[t, h, j, (k - 1) * RH:k * RH, :].astype(F32)
        produced = (xg[t, j, 0, h].astype(F32) + branch).astype(BF16)
        out[t, h * RH:(h + 1) * RH, j * CW:(j + 1) * CW] = produced

        @pl.when((t < T - 1) & (pipe < NP - 1))
        def _():
            shift_copy(t, h, j).start()

    for j in range(J):
        spread_all(0, j)
    await_bytes(gain, g_sem)
    clear(0)

    def opening(j, c):
        loaded(j)
        project_all(0, j)
        return c

    lax.fori_loop(0, J - 1, opening, 0)
    loaded(J - 1)
    last_all(0)

    def close(t, more):
        for h in range(H - 1):
            for j in range(J):
                finish(t, h, j)
        for j in range(J):
            finish(t, H - 1, j)
            if H > 1:
                @pl.when(more)
                def _():
                    spread(t + 1, 0, j)
        if H == 1:
            @pl.when(more)
            def _():
                for j in range(J):
                    spread(t + 1, 0, j)

    for h in range(H):
        contract(0, h)
    for j in range(J):
        turn(j)
    close(0, T > 1)

    def tick(t, carry):
        clear(t)

        def first(j, c):
            if H > 1:
                spread(t, 1, j)
            project(t, 0, j)
            return c

        lax.fori_loop(0, J - 1, first, 0)
        if H > 1:
            spread(t, 1, J - 1)
        project_last(t, 0)
        if H > 1:
            def second(j, c):
                project(t, 1, j)
                return c

            lax.fori_loop(0, BEFORE, second, 0)
            contract(t, 0)
            lax.fori_loop(BEFORE, J - 1, second, 0)
            project_last(t, 1)
        contract(t, H - 1)
        close(t, t < T - 1)
        return carry

    lax.fori_loop(1, T, tick, 0)

    for j in range(J):
        await_bytes(xg.at[0, j, pl.ds(1, NT - 1)], ag_s.at[0, 0, j])

    def sent(t, carry):
        for h in range(H):
            for j in range(J):
                @pl.when(t > 0)
                def _():
                    await_bytes(others(t, h, j), ag_s.at[t, h, j])

                await_bytes(rs_recv.at[t, h, j], rs_s.at[t, h, j])

                @pl.when((t < T - 1) & (pipe < NP - 1))
                def _():
                    shift_copy(t, h, j).wait_send()
            for k in range(1, NS):
                squares_copy(t, h, k).wait_send()
                for n in range(NF):
                    exchange_copy(t, h, n, k).wait_send()
        return carry

    lax.fori_loop(0, T, sent, 0)


def solution(mesh):
    NP, NS, NT = mesh.shape["pipe"], mesh.shape["seq"], mesh.shape["tp"]

    def shards(in_flight, arriving, norm_gain, gate_weight, up_weight, down_weight):
        T = arriving.shape[0] + 1
        R, DL = in_flight.shape[1:]
        F = gate_weight.shape[2]
        CW = min(COLUMNS, DL)
        J = DL // CW
        H = 2 if R % 32 == 0 else 1
        RH = R // H
        M = RH * NT
        parts = pieces(F, PART)
        NF = len(parts)
        cfg = (T, R, DL, F, CW, H, NP, NS, NT, parts)
        hbm = pl.BlockSpec(memory_space=pltpu.HBM)
        vmem = pl.BlockSpec(memory_space=pltpu.VMEM)
        dma = pltpu.SemaphoreType.DMA
        ps = max(NS - 1, 1)
        scratch = [
            pltpu.VMEM((1, DL), BF16),
            pltpu.VMEM((T, J, NT, H, RH, CW), BF16),
            pltpu.VMEM((J, F, CW), BF16),
            pltpu.VMEM((J, F, CW), BF16),
            pltpu.VMEM((J, CW, F), BF16),
            pltpu.VMEM((J, CW, F), BF16),
            pltpu.VMEM((F, DL), BF16),
            pltpu.VMEM((NT, H, RH, F), F32),
            pltpu.VMEM((NT, H, RH, F), F32),
            pltpu.VMEM((M, DL), F32),
            pltpu.VMEM((T, H, M, 128), F32),
            pltpu.VMEM((T, H, ps, M, 128), F32),
            pltpu.VMEM((T, H, J, M, CW), BF16),
            pltpu.VMEM((T, H, J, M - RH, CW), BF16),
        ]
        scratch += [pltpu.VMEM((T, H, 2, M, size), BF16) for _, size in parts]
        scratch += [pltpu.VMEM((T, H, ps, 2, M, size), BF16) for _, size in parts]
        scratch += [
            dma, dma((2, J)), dma((NF,)), dma((T, H, J)), dma((T, H, J)),
            dma((T, H, J)), dma((T, H, J)), dma((T, H, J)), dma((T, H, J)),
            dma((T, H, ps)), dma((T, H, ps)), dma((T, H, NF, ps)), dma((T, H, NF, ps)),
        ]
        flops = 2 * T * H * M * DL * F * 3
        made = pl.pallas_call(
            functools.partial(body, cfg),
            out_shape=pltpu.VMEM((T, R, DL), BF16),
            in_specs=[hbm, hbm, hbm, hbm, hbm, hbm],
            out_specs=vmem,
            scratch_shapes=scratch,
            compiler_params=pltpu.CompilerParams(
                collective_id=0, has_side_effects=True, vmem_limit_bytes=56 * 1024 * 1024
            ),
            cost_estimate=pl.CostEstimate(flops=flops, bytes_accessed=6 * DL * F, transcendentals=T * H * M * F),
            name="relay",
        )(in_flight, arriving, norm_gain, jnp.swapaxes(gate_weight, 1, 2), jnp.swapaxes(up_weight, 1, 2), down_weight)
        return made[:, None]

    placed = (
        P("pipe", "tp", "seq"),
        P(None, "tp", "seq"),
        P("pipe", "seq"),
        P("pipe", "seq", "tp"),
        P("pipe", "seq", "tp"),
        P("pipe", "tp", "seq"),
    )
    return jax.shard_map(
        shards, mesh=mesh, in_specs=placed, out_specs=P(None, "pipe", "tp", "seq"), check_vma=False
    )
```

```python
import functools

import jax
import jax.numpy as jnp
from jax import lax
from jax.experimental import pallas as pl
from jax.experimental.pallas import tpu as pltpu
from jax.sharding import PartitionSpec as P

epsilon = 1e-05
MESH = pl.DeviceIdType.MESH
F32, BF16 = jnp.float32, jnp.bfloat16
COLUMNS = 512
PART = 1408
BEFORE = 1


def pieces(total, step):
    return [(at, min(step, total - at)) for at in range(0, total, step)]


def times(a, b):
    return lax.dot_general(a, b, (((1,), (1,)), ((), ())), preferred_element_type=F32)


def partner(me, k, n):
    if n & (n - 1):
        raise ValueError("axis size")
    result, bit = 0, 1
    while bit < n:
        digit = (me // bit) % 2
        if k & bit:
            digit = 1 - digit
        result = result + digit * bit
        bit *= 2
    return result


def body(cfg, *refs):
    T, R, DL, F, CW, H, NP, NS, NT, parts = cfg
    J, RH, NF = DL // CW, R // H, len(parts)
    M = RH * NT
    refs = list(refs)
    in_flight, arriving, gain_in, gate_w, up_w, down_w, out = refs[:7]
    (gain, xg, gate_v, up_v, gate_t, up_t, down_v, acc_g, acc_u, acc_y, sq, sq_recv, rs_send, rs_recv) = refs[7:21]
    ex_send = refs[21:21 + NF]
    ex_recv = refs[21 + NF:21 + 2 * NF]
    (g_sem, w_sem, d_sem, x_sem, z_sem, ag_s, ag_r, rs_s, rs_r, sq_s, sq_r, ex_s, ex_r) = refs[21 + 2 * NF:]

    pipe, seq, tp = lax.axis_index("pipe"), lax.axis_index("seq"), lax.axis_index("tp")
    width = DL * NS

    def remote(src, dst, send, recv, where):
        return pltpu.make_async_remote_copy(
            src_ref=src, dst_ref=dst, send_sem=send, recv_sem=recv, device_id=where, device_id_type=MESH
        )

    def await_bytes(ref, sem):
        pltpu.make_async_copy(ref, ref, sem).wait()

    def own(t, h, j):
        return xg.at[t, j, 0, h]

    def others(t, h, j):
        return xg.at[t, j, pl.ds(1, NT - 1), h]

    for j in range(J):
        for h in range(H):
            pltpu.make_async_copy(
                in_flight.at[0, pl.ds(h * RH, RH), pl.ds(j * CW, CW)], own(0, h, j), x_sem.at[0, h, j]
            ).start()
    pltpu.make_async_copy(gain_in, gain, g_sem).start()
    for j in range(J):
        for which, (src, dst) in enumerate(((gate_w, gate_v), (up_w, up_v))):
            pltpu.make_async_copy(src.at[0, :, pl.ds(j * CW, CW)], dst.at[j], w_sem.at[which, j]).start()
    for n, (at, size) in enumerate(parts):
        pltpu.make_async_copy(down_w.at[0, pl.ds(at, size), :], down_v.at[pl.ds(at, size), :], d_sem.at[n]).start()

    @pl.when(pipe == 0)
    def _():
        for t in range(1, T):
            for h in range(H):
                for j in range(J):
                    pltpu.make_async_copy(
                        arriving.at[t - 1, pl.ds(h * RH, RH), pl.ds(j * CW, CW)], own(t, h, j), x_sem.at[t, h, j]
                    ).start()

    barrier = pltpu.get_barrier_semaphore()
    for k in range(1, NT):
        pl.semaphore_signal(barrier, inc=1, device_id={"tp": partner(tp, k, NT)}, device_id_type=MESH)
    for k in range(1, NS):
        pl.semaphore_signal(barrier, inc=1, device_id={"seq": partner(seq, k, NS)}, device_id_type=MESH)

    @pl.when(pipe > 0)
    def _():
        pl.semaphore_signal(barrier, inc=1, device_id={"pipe": pipe - 1}, device_id_type=MESH)

    peers = NT - 1 + NS - 1

    @pl.when(pipe < NP - 1)
    def _():
        pl.semaphore_wait(barrier, peers + 1)

    @pl.when(pipe == NP - 1)
    def _():
        pl.semaphore_wait(barrier, peers)

    def spread(t, h, j):
        await_bytes(own(t, h, j), x_sem.at[t, h, j])
        for k in reversed(range(1, NT)):
            remote(
                own(t, h, j), xg.at[t, j, k, h], ag_s.at[t, h, j], ag_r.at[t, h, j], {"tp": partner(tp, k, NT)}
            ).start()

    def spread_all(t, j):
        for h in range(H):
            await_bytes(own(t, h, j), x_sem.at[t, h, j])
        for k in reversed(range(1, NT)):
            remote(
                xg.at[t, j, 0], xg.at[t, j, k], ag_s.at[t, 0, j], ag_r.at[t, 0, j], {"tp": partner(tp, k, NT)}
            ).start()

    def shift_copy(t, h, j):
        return remote(
            out.at[t, pl.ds(h * RH, RH), pl.ds(j * CW, CW)], own(t + 1, h, j), z_sem.at[t, h, j],
            x_sem.at[t + 1, h, j], {"pipe": pipe + 1},
        )

    def squares_copy(t, h, k):
        return remote(
            sq.at[t, h], sq_recv.at[t, h, k - 1], sq_s.at[t, h, k - 1], sq_r.at[t, h, k - 1],
            {"seq": partner(seq, k, NS)},
        )

    def exchange_copy(t, h, n, k):
        return remote(
            ex_send[n].at[t, h], ex_recv[n].at[t, h, k - 1], ex_s.at[t, h, n, k - 1], ex_r.at[t, h, n, k - 1],
            {"seq": partner(seq, k, NS)},
        )

    def scale(x, j):
        wide = x.astype(F32)
        scaled = (wide * gain[:, pl.ds(pl.multiple_of(j * CW, CW), CW)].astype(F32)).astype(BF16)
        square = wide * wide
        total = square[:, 0:128]
        for at in range(128, CW, 128):
            total = total + square[:, at:at + 128]
        return scaled, total

    def turn(j):
        for which, (raw, turned) in enumerate(((gate_v, gate_t), (up_v, up_t))):
            for at in range(0, CW, 256):
                turned[j, at:at + 256, :] = jnp.transpose(raw[j, :, at:at + 256])

    def arrive_all(t, j):
        await_bytes(xg.at[t, j, pl.ds(1, NT - 1)], ag_r.at[t, 0, j])
        scaled, total = scale(xg[t, j].reshape(H * M, CW), j)
        total = total.reshape(NT, H, RH, 128)
        for h in range(H):
            sq[t, h] += total[:, h].reshape(M, 128)
        return scaled

    def arrive(t, h, j):
        await_bytes(others(t, h, j), ag_r.at[t, h, j])
        scaled, total = scale(xg[t, j, :, h].reshape(M, CW), j)
        sq[t, h] += total
        return scaled

    kinds = ((gate_t, acc_g), (up_t, acc_u))
    raws = ((gate_v, acc_g), (up_v, acc_u))

    def loaded(j):
        await_bytes(gate_v.at[j], w_sem.at[0, j])
        await_bytes(up_v.at[j], w_sem.at[1, j])

    def clear(t):
        acc_g[...] = jnp.zeros_like(acc_g)
        acc_u[...] = jnp.zeros_like(acc_u)
        for h in range(H):
            sq[t, h] = jnp.zeros((M, 128), F32)

    def project_all(t, j):
        scaled = arrive_all(t, j)
        for at, size in pieces(F, 256):
            for weight, acc in raws:
                acc[:, :, :, at:at + size] += times(scaled, weight[j, at:at + size, :]).reshape(NT, H, RH, size)

    def project(t, h, j):
        scaled = arrive(t, h, j)
        for at, size in pieces(F, 256):
            for weight, acc in kinds:
                acc[:, h, :, at:at + size] += jnp.dot(
                    scaled, weight[j, :, at:at + size], preferred_element_type=F32
                ).reshape(NT, RH, size)

    def last_all(t):
        scaled = arrive_all(t, J - 1)
        for h in range(H):
            for k in range(1, NS):
                squares_copy(t, h, k).start()
        for n, (base, length) in enumerate(parts):
            for at, size in pieces(length, 256):
                lo, hi = base + at, base + at + size
                for which, (weight, acc) in enumerate(raws):
                    value = acc[:, :, :, lo:hi] + times(scaled, weight[J - 1, lo:hi, :]).reshape(NT, H, RH, size)
                    acc[:, :, :, lo:hi] = value
                    rounded = value.astype(BF16)
                    for h in range(H):
                        ex_send[n][t, h, which, :, at:at + size] = rounded[:, h].reshape(M, size)
            for h in range(H):
                for k in range(1, NS):
                    exchange_copy(t, h, n, k).start()

    def project_last(t, h):
        scaled = arrive(t, h, J - 1)
        for k in range(1, NS):
            squares_copy(t, h, k).start()
        for n, (base, length) in enumerate(parts):
            for at, size in pieces(length, 256):
                lo, hi = base + at, base + at + size
                for which, (weight, acc) in enumerate(kinds):
                    value = acc[:, h, :, lo:hi].reshape(M, size) + jnp.dot(
                        scaled, weight[J - 1, :, lo:hi], preferred_element_type=F32
                    )
                    acc[:, h, :, lo:hi] = value.reshape(NT, RH, size)
                    ex_send[n][t, h, which, :, at:at + size] = value.astype(BF16)
            for k in range(1, NS):
                exchange_copy(t, h, n, k).start()

    def contract(t, h):
        total = sq[t, h]
        for k in range(1, NS):
            await_bytes(sq_recv.at[t, h, k - 1], sq_r.at[t, h, k - 1])
            total = total + sq_recv[t, h, k - 1]
        inverse = lax.rsqrt(jnp.sum(total, axis=1, keepdims=True) / width + epsilon)
        for n, (base, length) in enumerate(parts):
            for k in range(1, NS):
                await_bytes(ex_recv[n].at[t, h, k - 1], ex_r.at[t, h, n, k - 1])
            if h == 0 and isinstance(t, int):
                await_bytes(down_v.at[pl.ds(base, length), :], d_sem.at[n])
            gate = acc_g[:, h, :, base:base + length].reshape(M, length)
            up = acc_u[:, h, :, base:base + length].reshape(M, length)
            for k in range(1, NS):
                gate = gate + ex_recv[n][t, h, k - 1, 0].astype(F32)
                up = up + ex_recv[n][t, h, k - 1, 1].astype(F32)
            hidden = (jax.nn.silu(gate * inverse) * (up * inverse)).astype(BF16)
            last = n == NF - 1
            for j in range(J):
                for at, size in pieces(CW, 256):
                    lo = j * CW + at
                    value = jnp.dot(hidden, down_v[base:base + length, lo:lo + size], preferred_element_type=F32)
                    if n > 0:
                        value = value + acc_y[:, lo:lo + size]
                    if last:
                        rs_send[t, h, j, :, at:at + size] = value.astype(BF16)
                    else:
                        acc_y[:, lo:lo + size] = value
                if last:
                    for k in reversed(range(1, NT)):
                        remote(
                            rs_send.at[t, h, j, pl.ds(k * RH, RH), :], rs_recv.at[t, h, j, pl.ds((k - 1) * RH, RH), :],
                            rs_s.at[t, h, j], rs_r.at[t, h, j], {"tp": partner(tp, k, NT)},
                        ).start()

    def finish(t, h, j):
        await_bytes(rs_recv.at[t, h, j], rs_r.at[t, h, j])
        branch = rs_send[t, h, j, 0:RH, :].astype(F32)
        for k in range(1, NT):
            branch = branch + rs_recv[t, h, j, (k - 1) * RH:k * RH, :].astype(F32)
        produced = (xg[t, j, 0, h].astype(F32) + branch).astype(BF16)
        out[t, h * RH:(h + 1) * RH, j * CW:(j + 1) * CW] = produced

        @pl.when((t < T - 1) & (pipe < NP - 1))
        def _():
            shift_copy(t, h, j).start()

    for j in range(J):
        spread_all(0, j)
    await_bytes(gain, g_sem)
    clear(0)

    def opening(j, c):
        loaded(j)
        project_all(0, j)
        return c

    lax.fori_loop(0, J - 1, opening, 0)
    loaded(J - 1)
    last_all(0)

    def close(t, more):
        for h in range(H - 1):
            for j in range(J):
                finish(t, h, j)
        for j in range(J):
            finish(t, H - 1, j)
            if H > 1:
                @pl.when(more)
                def _():
                    spread(t + 1, 0, j)
        if H == 1:
            @pl.when(more)
            def _():
                for j in range(J):
                    spread(t + 1, 0, j)

    for j in range(J // 4):
        turn(j)
    for h in range(H):
        contract(0, h)
    for j in range(J // 4, J):
        turn(j)
    close(0, T > 1)

    def tick(t, carry):
        clear(t)

        def first(j, c):
            project(t, 0, j)
            return c

        if H > 1:
            for j in range(J):
                spread(t, 1, j)
        for j in range(J - 1):
            first(j, 0)
        project_last(t, 0)
        if H > 1:
            def second(j, c):
                project(t, 1, j)
                return c

            [second(j, 0) for j in range(J - 1)]
            project_last(t, 1)
            contract(t, 0)
        contract(t, H - 1)
        close(t, t < T - 1)
        return carry

    lax.fori_loop(1, T, tick, 0)

    for j in range(J):
        await_bytes(xg.at[0, j, pl.ds(1, NT - 1)], ag_s.at[0, 0, j])

    def sent(t, carry):
        for h in range(H):
            for j in range(J):
                @pl.when(t > 0)
                def _():
                    await_bytes(others(t, h, j), ag_s.at[t, h, j])

                await_bytes(rs_recv.at[t, h, j], rs_s.at[t, h, j])

                @pl.when((t < T - 1) & (pipe < NP - 1))
                def _():
                    shift_copy(t, h, j).wait_send()
            for k in range(1, NS):
                squares_copy(t, h, k).wait_send()
                for n in range(NF):
                    exchange_copy(t, h, n, k).wait_send()
        return carry

    lax.fori_loop(0, T, sent, 0)


def solution(mesh):
    NP, NS, NT = mesh.shape["pipe"], mesh.shape["seq"], mesh.shape["tp"]

    def shards(in_flight, arriving, norm_gain, gate_weight, up_weight, down_weight):
        T = arriving.shape[0] + 1
        R, DL = in_flight.shape[1:]
        F = gate_weight.shape[2]
        CW = min(COLUMNS, DL)
        J = DL // CW
        H = 2 if R % 32 == 0 else 1
        RH = R // H
        M = RH * NT
        parts = pieces(F, PART)
        NF = len(parts)
        cfg = (T, R, DL, F, CW, H, NP, NS, NT, parts)
        hbm = pl.BlockSpec(memory_space=pltpu.HBM)
        vmem = pl.BlockSpec(memory_space=pltpu.VMEM)
        dma = pltpu.SemaphoreType.DMA
        ps = max(NS - 1, 1)
        scratch = [
            pltpu.VMEM((1, DL), BF16),
            pltpu.VMEM((T, J, NT, H, RH, CW), BF16),
            pltpu.VMEM((J, F, CW), BF16),
            pltpu.VMEM((J, F, CW), BF16),
            pltpu.VMEM((J, CW, F), BF16),
            pltpu.VMEM((J, CW, F), BF16),
            pltpu.VMEM((F, DL), BF16),
            pltpu.VMEM((NT, H, RH, F), F32),
            pltpu.VMEM((NT, H, RH, F), F32),
            pltpu.VMEM((M, DL), F32),
            pltpu.VMEM((T, H, M, 128), F32),
            pltpu.VMEM((T, H, ps, M, 128), F32),
            pltpu.VMEM((T, H, J, M, CW), BF16),
            pltpu.VMEM((T, H, J, M - RH, CW), BF16),
        ]
        scratch += [pltpu.VMEM((T, H, 2, M, size), BF16) for _, size in parts]
        scratch += [pltpu.VMEM((T, H, ps, 2, M, size), BF16) for _, size in parts]
        scratch += [
            dma, dma((2, J)), dma((NF,)), dma((T, H, J)), dma((T, H, J)),
            dma((T, H, J)), dma((T, H, J)), dma((T, H, J)), dma((T, H, J)),
            dma((T, H, ps)), dma((T, H, ps)), dma((T, H, NF, ps)), dma((T, H, NF, ps)),
        ]
        flops = 2 * T * H * M * DL * F * 3
        made = pl.pallas_call(
            functools.partial(body, cfg),
            out_shape=pltpu.VMEM((T, R, DL), BF16),
            in_specs=[hbm, hbm, hbm, hbm, hbm, hbm],
            out_specs=vmem,
            scratch_shapes=scratch,
            compiler_params=pltpu.CompilerParams(
                collective_id=0, has_side_effects=True, vmem_limit_bytes=56 * 1024 * 1024
            ),
            cost_estimate=pl.CostEstimate(flops=flops, bytes_accessed=6 * DL * F, transcendentals=T * H * M * F),
            name="relay",
        )(in_flight, arriving, norm_gain, jnp.swapaxes(gate_weight, 1, 2), jnp.swapaxes(up_weight, 1, 2), down_weight)
        return made[:, None]

    placed = (
        P("pipe", "tp", "seq"),
        P(None, "tp", "seq"),
        P("pipe", "seq"),
        P("pipe", "seq", "tp"),
        P("pipe", "seq", "tp"),
        P("pipe", "tp", "seq"),
    )
    return jax.shard_map(
        shards, mesh=mesh, in_specs=placed, out_specs=P(None, "pipe", "tp", "seq"), check_vma=False
    )
```

```python
import functools

import jax
import jax.numpy as jnp
from jax import lax
from jax.experimental import pallas as pl
from jax.experimental.pallas import tpu as pltpu
from jax.sharding import PartitionSpec as P

epsilon = 1e-05
MESH = pl.DeviceIdType.MESH
F32, BF16 = jnp.float32, jnp.bfloat16
COLUMNS = 512
PART = 1408
BEFORE = 1


def pieces(total, step):
    return [(at, min(step, total - at)) for at in range(0, total, step)]


def times(a, b):
    return lax.dot_general(a, b, (((1,), (1,)), ((), ())), preferred_element_type=F32)


def partner(me, k, n):
    if n & (n - 1):
        raise ValueError("axis size")
    result, bit = 0, 1
    while bit < n:
        digit = (me // bit) % 2
        if k & bit:
            digit = 1 - digit
        result = result + digit * bit
        bit *= 2
    return result


def body(cfg, *refs):
    T, R, DL, F, CW, H, NP, NS, NT, parts = cfg
    J, RH, NF = DL // CW, R // H, len(parts)
    M = RH * NT
    refs = list(refs)
    in_flight, arriving, gain_in, gate_w, up_w, down_w, out = refs[:7]
    (gain, xg, gate_v, up_v, gate_t, up_t, down_v, acc_g, acc_u, acc_y, sq, sq_recv, rs_send, rs_recv) = refs[7:21]
    ex_send = refs[21:21 + NF]
    ex_recv = refs[21 + NF:21 + 2 * NF]
    (g_sem, w_sem, d_sem, x_sem, z_sem, ag_s, ag_r, rs_s, rs_r, sq_s, sq_r, ex_s, ex_r) = refs[21 + 2 * NF:]

    pipe, seq, tp = lax.axis_index("pipe"), lax.axis_index("seq"), lax.axis_index("tp")
    width = DL * NS

    def remote(src, dst, send, recv, where):
        return pltpu.make_async_remote_copy(
            src_ref=src, dst_ref=dst, send_sem=send, recv_sem=recv, device_id=where, device_id_type=MESH
        )

    def await_bytes(ref, sem):
        pltpu.make_async_copy(ref, ref, sem).wait()

    def own(t, h, j):
        return xg.at[t, j, 0, h]

    def others(t, h, j):
        return xg.at[t, j, pl.ds(1, NT - 1), h]

    for j in range(J):
        for h in range(H):
            pltpu.make_async_copy(
                in_flight.at[0, pl.ds(h * RH, RH), pl.ds(j * CW, CW)], own(0, h, j), x_sem.at[0, h, j]
            ).start()
    pltpu.make_async_copy(gain_in, gain, g_sem).start()
    for j in range(J):
        for which, (src, dst) in enumerate(((gate_w, gate_v), (up_w, up_v))):
            pltpu.make_async_copy(src.at[0, :, pl.ds(j * CW, CW)], dst.at[j], w_sem.at[which, j]).start()
    for n, (at, size) in enumerate(parts):
        pltpu.make_async_copy(down_w.at[0, pl.ds(at, size), :], down_v.at[pl.ds(at, size), :], d_sem.at[n]).start()

    @pl.when(pipe == 0)
    def _():
        for t in range(1, T):
            for h in range(H):
                for j in range(J):
                    pltpu.make_async_copy(
                        arriving.at[t - 1, pl.ds(h * RH, RH), pl.ds(j * CW, CW)], own(t, h, j), x_sem.at[t, h, j]
                    ).start()

    barrier = pltpu.get_barrier_semaphore()
    for k in range(1, NT):
        pl.semaphore_signal(barrier, inc=1, device_id={"tp": partner(tp, k, NT)}, device_id_type=MESH)
    for k in range(1, NS):
        pl.semaphore_signal(barrier, inc=1, device_id={"seq": partner(seq, k, NS)}, device_id_type=MESH)

    @pl.when(pipe > 0)
    def _():
        pl.semaphore_signal(barrier, inc=1, device_id={"pipe": pipe - 1}, device_id_type=MESH)

    peers = NT - 1 + NS - 1

    @pl.when(pipe < NP - 1)
    def _():
        pl.semaphore_wait(barrier, peers + 1)

    @pl.when(pipe == NP - 1)
    def _():
        pl.semaphore_wait(barrier, peers)

    def spread(t, h, j):
        await_bytes(own(t, h, j), x_sem.at[t, h, j])
        for k in reversed(range(1, NT)):
            remote(
                own(t, h, j), xg.at[t, j, k, h], ag_s.at[t, h, j], ag_r.at[t, h, j], {"tp": partner(tp, k, NT)}
            ).start()

    def spread_all(t, j):
        for h in range(H):
            await_bytes(own(t, h, j), x_sem.at[t, h, j])
        for k in reversed(range(1, NT)):
            remote(
                xg.at[t, j, 0], xg.at[t, j, k], ag_s.at[t, 0, j], ag_r.at[t, 0, j], {"tp": partner(tp, k, NT)}
            ).start()

    def shift_copy(t, h, j):
        return remote(
            out.at[t, pl.ds(h * RH, RH), pl.ds(j * CW, CW)], own(t + 1, h, j), z_sem.at[t, h, j],
            x_sem.at[t + 1, h, j], {"pipe": pipe + 1},
        )

    def squares_copy(t, h, k):
        return remote(
            sq.at[t, h], sq_recv.at[t, h, k - 1], sq_s.at[t, h, k - 1], sq_r.at[t, h, k - 1],
            {"seq": partner(seq, k, NS)},
        )

    def exchange_copy(t, h, n, k):
        return remote(
            ex_send[n].at[t, h], ex_recv[n].at[t, h, k - 1], ex_s.at[t, h, n, k - 1], ex_r.at[t, h, n, k - 1],
            {"seq": partner(seq, k, NS)},
        )

    def scale(x, j):
        wide = x.astype(F32)
        scaled = (wide * gain[:, pl.ds(pl.multiple_of(j * CW, CW), CW)].astype(F32)).astype(BF16)
        square = wide * wide
        total = square[:, 0:128]
        for at in range(128, CW, 128):
            total = total + square[:, at:at + 128]
        return scaled, total

    def turn(j):
        for which, (raw, turned) in enumerate(((gate_v, gate_t), (up_v, up_t))):
            for at in range(0, CW, 256):
                turned[j, at:at + 256, :] = jnp.transpose(raw[j, :, at:at + 256])

    def arrive_all(t, j):
        await_bytes(xg.at[t, j, pl.ds(1, NT - 1)], ag_r.at[t, 0, j])
        scaled, total = scale(xg[t, j].reshape(H * M, CW), j)
        total = total.reshape(NT, H, RH, 128)
        for h in range(H):
            sq[t, h] += total[:, h].reshape(M, 128)
        return scaled

    def arrive(t, h, j):
        await_bytes(others(t, h, j), ag_r.at[t, h, j])
        scaled, total = scale(xg[t, j, :, h].reshape(M, CW), j)
        sq[t, h] += total
        return scaled

    kinds = ((gate_t, acc_g), (up_t, acc_u))
    raws = ((gate_v, acc_g), (up_v, acc_u))

    def loaded(j):
        await_bytes(gate_v.at[j], w_sem.at[0, j])
        await_bytes(up_v.at[j], w_sem.at[1, j])

    def clear(t):
        acc_g[...] = jnp.zeros_like(acc_g)
        acc_u[...] = jnp.zeros_like(acc_u)
        for h in range(H):
            sq[t, h] = jnp.zeros((M, 128), F32)

    def project_all(t, j):
        scaled = arrive_all(t, j)
        for at, size in pieces(F, 256):
            for weight, acc in raws:
                acc[:, :, :, at:at + size] += times(scaled, weight[j, at:at + size, :]).reshape(NT, H, RH, size)

    def project(t, h, j):
        scaled = arrive(t, h, j)
        for at, size in pieces(F, 256):
            for weight, acc in kinds:
                acc[:, h, :, at:at + size] += jnp.dot(
                    scaled, weight[j, :, at:at + size], preferred_element_type=F32
                ).reshape(NT, RH, size)

    def last_all(t):
        scaled = arrive_all(t, J - 1)
        for h in range(H):
            for k in range(1, NS):
                squares_copy(t, h, k).start()
        for n, (base, length) in enumerate(parts):
            for at, size in pieces(length, 256):
                lo, hi = base + at, base + at + size
                for which, (weight, acc) in enumerate(raws):
                    value = acc[:, :, :, lo:hi] + times(scaled, weight[J - 1, lo:hi, :]).reshape(NT, H, RH, size)
                    acc[:, :, :, lo:hi] = value
                    rounded = value.astype(BF16)
                    for h in range(H):
                        ex_send[n][t, h, which, :, at:at + size] = rounded[:, h].reshape(M, size)
            for h in range(H):
                for k in range(1, NS):
                    exchange_copy(t, h, n, k).start()

    def project_last(t, h):
        scaled = arrive(t, h, J - 1)
        for k in range(1, NS):
            squares_copy(t, h, k).start()
        for n, (base, length) in enumerate(parts):
            for at, size in pieces(length, 256):
                lo, hi = base + at, base + at + size
                for which, (weight, acc) in enumerate(kinds):
                    value = acc[:, h, :, lo:hi].reshape(M, size) + jnp.dot(
                        scaled, weight[J - 1, :, lo:hi], preferred_element_type=F32
                    )
                    acc[:, h, :, lo:hi] = value.reshape(NT, RH, size)
                    ex_send[n][t, h, which, :, at:at + size] = value.astype(BF16)
            for k in range(1, NS):
                exchange_copy(t, h, n, k).start()

    def contract(t, h):
        total = sq[t, h]
        for k in range(1, NS):
            await_bytes(sq_recv.at[t, h, k - 1], sq_r.at[t, h, k - 1])
            total = total + sq_recv[t, h, k - 1]
        inverse = lax.rsqrt(jnp.sum(total, axis=1, keepdims=True) / width + epsilon)
        for n, (base, length) in enumerate(parts):
            for k in range(1, NS):
                await_bytes(ex_recv[n].at[t, h, k - 1], ex_r.at[t, h, n, k - 1])
            if h == 0 and isinstance(t, int):
                await_bytes(down_v.at[pl.ds(base, length), :], d_sem.at[n])
            gate = acc_g[:, h, :, base:base + length].reshape(M, length)
            up = acc_u[:, h, :, base:base + length].reshape(M, length)
            for k in range(1, NS):
                gate = gate + ex_recv[n][t, h, k - 1, 0].astype(F32)
                up = up + ex_recv[n][t, h, k - 1, 1].astype(F32)
            hidden = (jax.nn.silu(gate * inverse) * (up * inverse)).astype(BF16)
            last = n == NF - 1
            for j in range(J):
                for at, size in pieces(CW, 512):
                    lo = j * CW + at
                    value = jnp.dot(hidden, down_v[base:base + length, lo:lo + size], preferred_element_type=F32)
                    if n > 0:
                        value = value + acc_y[:, lo:lo + size]
                    if last:
                        rs_send[t, h, j, :, at:at + size] = value.astype(BF16)
                    else:
                        acc_y[:, lo:lo + size] = value
                if last:
                    for k in reversed(range(1, NT)):
                        remote(
                            rs_send.at[t, h, j, pl.ds(k * RH, RH), :], rs_recv.at[t, h, j, pl.ds((k - 1) * RH, RH), :],
                            rs_s.at[t, h, j], rs_r.at[t, h, j], {"tp": partner(tp, k, NT)},
                        ).start()

    def finish(t, h, j):
        await_bytes(rs_recv.at[t, h, j], rs_r.at[t, h, j])
        branch = rs_send[t, h, j, 0:RH, :].astype(F32)
        for k in range(1, NT):
            branch = branch + rs_recv[t, h, j, (k - 1) * RH:k * RH, :].astype(F32)
        produced = (xg[t, j, 0, h].astype(F32) + branch).astype(BF16)
        out[t, h * RH:(h + 1) * RH, j * CW:(j + 1) * CW] = produced

        @pl.when((t < T - 1) & (pipe < NP - 1))
        def _():
            shift_copy(t, h, j).start()

    for j in range(J):
        spread_all(0, j)
    await_bytes(gain, g_sem)
    clear(0)

    def opening(j, c):
        loaded(j)
        project_all(0, j)
        return c

    lax.fori_loop(0, J - 1, opening, 0)
    loaded(J - 1)
    last_all(0)

    def close(t, more):
        for h in range(H - 1):
            for j in range(J):
                finish(t, h, j)
        for j in range(J):
            finish(t, H - 1, j)
            if H > 1:
                @pl.when(more)
                def _():
                    spread(t + 1, 0, j)
        if H == 1:
            @pl.when(more)
            def _():
                for j in range(J):
                    spread(t + 1, 0, j)

    for j in range(J // 4):
        turn(j)
    contract(0, 0)
    for j in range(J // 4, J // 2):
        turn(j)
    for h in range(1, H):
        contract(0, h)
    for j in range(J // 2, J):
        turn(j)
    close(0, T > 1)

    def tick(t, carry):
        clear(t)

        def first(j, c):
            project(t, 0, j)
            return c

        if H > 1:
            for j in range(J):
                spread(t, 1, j)
        for j in range(J - 1):
            first(j, 0)
        project_last(t, 0)
        if H > 1:
            def second(j, c):
                project(t, 1, j)
                return c

            [second(j, 0) for j in range(J - 1)]
            project_last(t, 1)
            contract(t, 0)
        contract(t, H - 1)
        close(t, t < T - 1)
        return carry

    lax.fori_loop(1, T, tick, 0)

    for j in range(J):
        await_bytes(xg.at[0, j, pl.ds(1, NT - 1)], ag_s.at[0, 0, j])

    def sent(t, carry):
        for h in range(H):
            for j in range(J):
                @pl.when(t > 0)
                def _():
                    await_bytes(others(t, h, j), ag_s.at[t, h, j])

                await_bytes(rs_recv.at[t, h, j], rs_s.at[t, h, j])

                @pl.when((t < T - 1) & (pipe < NP - 1))
                def _():
                    shift_copy(t, h, j).wait_send()
            for k in range(1, NS):
                squares_copy(t, h, k).wait_send()
                for n in range(NF):
                    exchange_copy(t, h, n, k).wait_send()
        return carry

    lax.fori_loop(0, T, sent, 0)


def solution(mesh):
    NP, NS, NT = mesh.shape["pipe"], mesh.shape["seq"], mesh.shape["tp"]

    def shards(in_flight, arriving, norm_gain, gate_weight, up_weight, down_weight):
        T = arriving.shape[0] + 1
        R, DL = in_flight.shape[1:]
        F = gate_weight.shape[2]
        CW = min(COLUMNS, DL)
        J = DL // CW
        H = 2 if R % 32 == 0 else 1
        RH = R // H
        M = RH * NT
        parts = pieces(F, PART)
        NF = len(parts)
        cfg = (T, R, DL, F, CW, H, NP, NS, NT, parts)
        hbm = pl.BlockSpec(memory_space=pltpu.HBM)
        vmem = pl.BlockSpec(memory_space=pltpu.VMEM)
        dma = pltpu.SemaphoreType.DMA
        ps = max(NS - 1, 1)
        scratch = [
            pltpu.VMEM((1, DL), BF16),
            pltpu.VMEM((T, J, NT, H, RH, CW), BF16),
            pltpu.VMEM((J, F, CW), BF16),
            pltpu.VMEM((J, F, CW), BF16),
            pltpu.VMEM((J, CW, F), BF16),
            pltpu.VMEM((J, CW, F), BF16),
            pltpu.VMEM((F, DL), BF16),
            pltpu.VMEM((NT, H, RH, F), F32),
            pltpu.VMEM((NT, H, RH, F), F32),
            pltpu.VMEM((M, DL), F32),
            pltpu.VMEM((T, H, M, 128), F32),
            pltpu.VMEM((T, H, ps, M, 128), F32),
            pltpu.VMEM((T, H, J, M, CW), BF16),
            pltpu.VMEM((T, H, J, M - RH, CW), BF16),
        ]
        scratch += [pltpu.VMEM((T, H, 2, M, size), BF16) for _, size in parts]
        scratch += [pltpu.VMEM((T, H, ps, 2, M, size), BF16) for _, size in parts]
        scratch += [
            dma, dma((2, J)), dma((NF,)), dma((T, H, J)), dma((T, H, J)),
            dma((T, H, J)), dma((T, H, J)), dma((T, H, J)), dma((T, H, J)),
            dma((T, H, ps)), dma((T, H, ps)), dma((T, H, NF, ps)), dma((T, H, NF, ps)),
        ]
        flops = 2 * T * H * M * DL * F * 3
        made = pl.pallas_call(
            functools.partial(body, cfg),
            out_shape=pltpu.VMEM((T, R, DL), BF16),
            in_specs=[hbm, hbm, hbm, hbm, hbm, hbm],
            out_specs=vmem,
            scratch_shapes=scratch,
            compiler_params=pltpu.CompilerParams(
                collective_id=0, has_side_effects=True, vmem_limit_bytes=56 * 1024 * 1024
            ),
            cost_estimate=pl.CostEstimate(flops=flops, bytes_accessed=6 * DL * F, transcendentals=T * H * M * F),
            name="relay",
        )(in_flight, arriving, norm_gain, jnp.swapaxes(gate_weight, 1, 2), jnp.swapaxes(up_weight, 1, 2), down_weight)
        return made[:, None]

    placed = (
        P("pipe", "tp", "seq"),
        P(None, "tp", "seq"),
        P("pipe", "seq"),
        P("pipe", "seq", "tp"),
        P("pipe", "seq", "tp"),
        P("pipe", "tp", "seq"),
    )
    return jax.shard_map(
        shards, mesh=mesh, in_specs=placed, out_specs=P(None, "pipe", "tp", "seq"), check_vma=False
    )
```
